512 devices in a mesh: row: 8 (over x, y_hi), col: 64 (over y_lo, z, core).
Axes of the slice: x: 4, y: 4 (y_hi: 2, y_lo: 2; y = y_hi * 2 + y_lo), z: 16, core: 2. Of those that a mesh axis runs over, the one named last changes fastest.
Arguments:
- trace_maps: bfloat16 [8, 64, 1280, 1280], P('row', 'col'), may hold values from -0.125 to 0.125
- sources: bfloat16 [8, 64, 1280, 256], P('row', 'col'), may hold values from -6 to 6
Outputs:
- traces: bfloat16 [8, 64, 1280, 256], P('row', 'col')
The draws below stay inside these ranges and needn't reach their ends.
All inputs are finite; a program needn't handle non-finite values.
Results may differ from the reference program's by a relative error of at most 0.007.
Values may be sent and summed in bfloat16 or wider, within the bound.
A program may use at most 64 MiB of HBM per device.

```python
import jax
import jax.numpy as jnp
from jax import lax

TR = 640
RHS = 256
ITERS = 8
GR = 8
GC = 64


def shard_levels(key, extent, cuts, least, high):
    factor_of = 1.0
    for dim, shards_of in cuts:
        heights = jax.random.uniform(jax.random.fold_in(jax.random.fold_in(key, 6), dim), (shards_of,), jnp.float32, least / len(cuts), high / len(cuts))
        factor_of = factor_of * jnp.repeat(jnp.exp(heights), extent[dim] // shards_of).reshape((-1,) + (1,) * (len(extent) - 1 - dim))
    return factor_of


def gaussian(own_key, extent, scale, bound, pieces=(), dtype=jnp.bfloat16):
    values = jax.random.normal(own_key, extent, jnp.float32) * scale
    if len(pieces) > 0:
        values = shard_levels(own_key, extent, pieces, -0.22, 0.18) * values
    return jnp.clip(values, min=-bound, max=bound).astype(dtype)


def setup_inputs(seed: int = 0) -> dict:
    key_list = jax.random.split(jax.random.key(seed), 3)
    return {
        "trace_maps": gaussian(key_list[0], (GR, GC, 2 * TR, 2 * TR), (4 * TR) ** -0.5, 0.125, ((0, 8), (1, 64))),
        "sources": gaussian(key_list[1], (GR, GC, 2 * TR, RHS), 1.0, 6.0, ((0, 8), (1, 64))),
    }


def apply_maps(maps_flat, incoming_flat):
    def one_block(pair):
        return jnp.dot(pair[0], pair[1], preferred_element_type=jnp.float32)
    return lax.map(one_block, (maps_flat, incoming_flat))


def reference(trace_maps, sources):
    rows_grid, cols_grid, order, width = sources.shape
    half = order // 2
    source_float = sources.astype(jnp.float32)
    state = source_float
    maps_flat = trace_maps.reshape(rows_grid * cols_grid, order, order)
    for step in range(ITERS):
        sent = state.astype(jnp.bfloat16)
        right = sent[:, :, :half]
        upper = sent[:, :, half:]
        left_in = jnp.concatenate([jnp.zeros_like(right[:, :1]), right[:, :-1]], axis=1)
        below_in = jnp.concatenate([jnp.zeros_like(upper[:1]), upper[:-1]], axis=0)
        incoming = jnp.concatenate([left_in, below_in], axis=2)
        product = apply_maps(maps_flat, incoming.reshape(rows_grid * cols_grid, order, width))
        state = product.reshape(rows_grid, cols_grid, order, width) + source_float
    return state.astype(jnp.bfloat16)
```

```python
import functools

import jax
import jax.numpy as jnp
from jax import lax
from jax.experimental import pallas as pl
from jax.experimental.pallas import tpu as pltpu
from jax.sharding import PartitionSpec as P

ITERS = 8
PARTS = 2
MESH = pl.DeviceIdType.MESH


def kernel(rows, cols, maps, sources, traces, mapping, state, left, below, total,
           load_sem, map_sem, right_sent, up_sent, left_got, below_got):
    half = left.shape[2]
    width = left.shape[3]
    row, col = lax.axis_index("row"), lax.axis_index("col")
    has_left, has_below = col > 0, row > 0
    has_right, has_above = col < cols - 1, row < rows - 1

    def lanes(part):
        return pl.ds(part * width, width)

    loads = [pltpu.make_async_copy(sources.at[0, 0, :, lanes(part)], state.at[0, part], load_sem.at[part])
             for part in range(PARTS)]
    for load in loads:
        load.start()
    map_load = pltpu.make_async_copy(maps.at[0, 0], mapping, map_sem)
    map_load.start()

    barrier = pltpu.get_barrier_semaphore()

    @pl.when(has_left)
    def _():
        pl.semaphore_signal(barrier, inc=1, device_id={"col": col - 1}, device_id_type=MESH)

    @pl.when(has_below)
    def _():
        pl.semaphore_signal(barrier, inc=1, device_id={"row": row - 1}, device_id_type=MESH)

    @pl.when(has_right | has_above)
    def _():
        pl.semaphore_wait(barrier, has_right.astype(jnp.int32) + has_above.astype(jnp.int32))

    def to_right(step, part):
        return pltpu.make_async_remote_copy(
            src_ref=state.at[step, part, pl.ds(0, half)], dst_ref=left.at[step, part],
            send_sem=right_sent.at[step, part], recv_sem=left_got.at[step, part],
            device_id={"col": lax.rem(col + 1, cols)}, device_id_type=MESH)

    def to_above(step, part):
        return pltpu.make_async_remote_copy(
            src_ref=state.at[step, part, pl.ds(half, half)], dst_ref=below.at[step, part],
            send_sem=up_sent.at[step, part], recv_sem=below_got.at[step, part],
            device_id={"row": lax.rem(row + 1, rows)}, device_id_type=MESH)

    for part in range(PARTS):
        loads[part].wait()

        @pl.when(has_above)
        def _():
            to_above(0, part).start()

        @pl.when(has_right)
        def _():
            to_right(0, part).start()

    @pl.when(jnp.logical_not(has_left))
    def _():
        left[ITERS] = jnp.zeros_like(left[ITERS])

    @pl.when(jnp.logical_not(has_below))
    def _():
        below[ITERS] = jnp.zeros_like(below[ITERS])

    map_load.wait()

    def advance(step, part, last):
        @pl.when(has_left)
        def _():
            to_right(step, part).wait_recv()

        total[...] = state[0, part].astype(jnp.float32) + jnp.dot(
            mapping[:, :half], left[jnp.where(has_left, step, ITERS), part],
            preferred_element_type=jnp.float32)

        @pl.when(has_below)
        def _():
            to_above(step, part).wait_recv()

        arrived = below[jnp.where(has_below, step, ITERS), part]
        upper = (total[half:] + jnp.dot(
            mapping[half:, half:], arrived, preferred_element_type=jnp.float32)).astype(jnp.bfloat16)
        if last:
            traces[0, 0, half:, part * width:(part + 1) * width] = upper
        else:
            state[step + 1, part, half:] = upper

            @pl.when(has_above)
            def _():
                to_above(step + 1, part).start()

        right = (total[:half] + jnp.dot(
            mapping[:half, half:], arrived, preferred_element_type=jnp.float32)).astype(jnp.bfloat16)
        if last:
            traces[0, 0, :half, part * width:(part + 1) * width] = right
        else:
            state[step + 1, part, :half] = right

            @pl.when(has_right)
            def _():
                to_right(step + 1, part).start()

    def one_step(step, carry):
        for part in range(PARTS):
            advance(step, part, False)
        return carry

    lax.fori_loop(0, ITERS - 1, one_step, 0)
    for part in range(PARTS):
        advance(ITERS - 1, part, True)

    def drain(step, carry):
        for part in range(PARTS):
            @pl.when(has_above)
            def _():
                to_above(step, part).wait_send()

            @pl.when(has_right)
            def _():
                to_right(step, part).wait_send()
        return carry

    lax.fori_loop(0, ITERS, drain, 0)


def per_device(rows, cols, trace_maps, sources):
    order, count = sources.shape[2:]
    half, width = order // 2, count // PARTS
    bf16, dma = jnp.bfloat16, pltpu.SemaphoreType.DMA
    return pl.pallas_call(
        functools.partial(kernel, rows, cols),
        out_shape=jax.ShapeDtypeStruct(sources.shape, bf16),
        in_specs=[pl.BlockSpec(memory_space=pltpu.HBM)] * 2,
        out_specs=pl.BlockSpec(memory_space=pltpu.VMEM),
        scratch_shapes=[
            pltpu.VMEM((order, order), bf16),
            pltpu.VMEM((ITERS, PARTS, order, width), bf16),
            pltpu.VMEM((ITERS + 1, PARTS, half, width), bf16),
            pltpu.VMEM((ITERS + 1, PARTS, half, width), bf16),
            pltpu.VMEM((order, width), jnp.float32),
            dma((PARTS,)),
            dma,
            dma((ITERS, PARTS)),
            dma((ITERS, PARTS)),
            dma((ITERS, PARTS)),
            dma((ITERS, PARTS)),
        ],
        compiler_params=pltpu.CompilerParams(
            collective_id=0, has_side_effects=True, vmem_limit_bytes=60 << 20),
    )(trace_maps, sources)


def solution(mesh):
    placed = P("row", "col", None, None)
    return jax.shard_map(
        functools.partial(per_device, mesh.shape["row"], mesh.shape["col"]),
        mesh=mesh,
        in_specs=(placed, placed),
        out_specs=placed,
        check_vma=False,
    )
```

```python
import functools

import jax
import jax.numpy as jnp
from jax import lax
from jax.experimental import pallas as pl
from jax.experimental.pallas import tpu as pltpu
from jax.sharding import PartitionSpec as P

ITERS = 8
RUN = 32
PIECES = ((0, 2, 112, 0, 1), (13, 15, 112, 224, 0), (2, 3, 96, 448, 1), (12, 13, 96, 544, 0))
PARTS = 2
MESH = pl.DeviceIdType.MESH


def kernel(rows, cols, maps, sources, traces, mapping, state, left, below, seam, total,
           load_sem, map_sem, right_sent, up_sent, left_got, below_got, seam_sent, seam_got):
    half = left.shape[2]
    width = left.shape[3]
    row, col = lax.axis_index("row"), lax.axis_index("col")
    has_left, has_below = col > 0, row > 0
    has_right, has_above = col < cols - 1, row < rows - 1
    before_seam, after_seam = col == RUN - 1, col == RUN
    chip = (col - RUN) // 2
    passes = [(col % 2 == core) & (chip >= max(first, 1)) & (chip < end) for first, end, _, _, core in PIECES]
    on_seam = functools.reduce(jnp.logical_or, passes)

    def lanes(part):
        return pl.ds(part * width, width)

    loads = [pltpu.make_async_copy(sources.at[0, 0, :, lanes(part)], state.at[0, part], load_sem.at[part])
             for part in range(PARTS)]
    for load in loads:
        load.start()
    map_load = pltpu.make_async_copy(maps.at[0, 0], mapping, map_sem)
    map_load.start()

    barrier = pltpu.get_barrier_semaphore()

    @pl.when(has_left)
    def _():
        pl.semaphore_signal(barrier, inc=1, device_id={"col": col - 1}, device_id_type=MESH)

    @pl.when(has_below)
    def _():
        pl.semaphore_signal(barrier, inc=1, device_id={"row": row - 1}, device_id_type=MESH)

    @pl.when(on_seam)
    def _():
        pl.semaphore_signal(barrier, inc=1, device_id={"col": RUN - 1}, device_id_type=MESH)

    @pl.when(after_seam)
    def _():
        for first, end, _, _, core in PIECES:
            for other in range(max(first, 1), end):
                pl.semaphore_signal(barrier, inc=1, device_id={"col": RUN + core + 2 * other}, device_id_type=MESH)

    @pl.when(has_right | has_above | on_seam)
    def _():
        pl.semaphore_wait(barrier, has_right.astype(jnp.int32) + has_above.astype(jnp.int32)
                          + on_seam.astype(jnp.int32) + (sum(end - first for first, end, *_ in PIECES) - 1) * before_seam.astype(jnp.int32))

    def to_right(step, part):
        return pltpu.make_async_remote_copy(
            src_ref=state.at[step, part, pl.ds(0, half)], dst_ref=left.at[step, part],
            send_sem=right_sent.at[step, part], recv_sem=left_got.at[step, part],
            device_id={"col": lax.rem(col + 1, cols)}, device_id_type=MESH)

    def to_above(step, part):
        return pltpu.make_async_remote_copy(
            src_ref=state.at[step, part, pl.ds(half, half)], dst_ref=below.at[step, part],
            send_sem=up_sent.at[step, part], recv_sem=below_got.at[step, part],
            device_id={"row": lax.rem(row + 1, rows)}, device_id_type=MESH)

    def straight(step, part):
        tall = PIECES[0][2]
        return pltpu.make_async_remote_copy(
            src_ref=state.at[step, part, pl.ds(0, tall)], dst_ref=left.at[step, part, pl.ds(0, tall)],
            send_sem=right_sent.at[step, part], recv_sem=left_got.at[step, part],
            device_id={"col": RUN}, device_id_type=MESH)

    def rows_of(kind, other):
        first, _, tall, start, _ = PIECES[kind]
        return pl.ds(pl.multiple_of(start + (other - first) * tall, 8), tall)

    def to_seam(step, part, kind, other):
        return pltpu.make_async_remote_copy(
            src_ref=state.at[step, part, rows_of(kind, other)],
            dst_ref=seam.at[step, part, pl.ds(0, PIECES[kind][2])],
            send_sem=right_sent.at[step, part], recv_sem=seam_got.at[step, part],
            device_id={"col": RUN + PIECES[kind][4] + 2 * other}, device_id_type=MESH)

    def from_seam(step, part, kind):
        return pltpu.make_async_remote_copy(
            src_ref=seam.at[step, part, pl.ds(0, PIECES[kind][2])],
            dst_ref=left.at[step, part, rows_of(kind, chip)],
            send_sem=seam_sent.at[step, part], recv_sem=left_got.at[step, part],
            device_id={"col": RUN}, device_id_type=MESH)

    def send_right(step, part):
        @pl.when(has_right & jnp.logical_not(before_seam))
        def _():
            to_right(step, part).start()

        @pl.when(before_seam)
        def _():
            for kind in reversed(range(len(PIECES))):
                def send(other, carry):
                    to_seam(step, part, kind, other).start()
                    return carry

                lax.fori_loop(max(PIECES[kind][0], 1), PIECES[kind][1], send, 0)
            straight(step, part).start()

    def pass_on(step, part):
        for kind in range(len(PIECES)):
            @pl.when(passes[kind])
            def _():
                to_seam(step, part, kind, chip).wait_recv()
                from_seam(step, part, kind).start()

    for part in range(PARTS):
        loads[part].wait()

        @pl.when(has_above)
        def _():
            to_above(0, part).start()

        send_right(0, part)

    @pl.when(jnp.logical_not(has_left))
    def _():
        left[ITERS] = jnp.zeros_like(left[ITERS])

    @pl.when(jnp.logical_not(has_below))
    def _():
        below[ITERS] = jnp.zeros_like(below[ITERS])

    map_load.wait()

    for part in range(PARTS):
        pass_on(0, part)

    def advance(step, part, last):
        @pl.when(has_left)
        def _():
            to_right(step, part).wait_recv()

        total[...] = state[0, part].astype(jnp.float32) + jnp.dot(
            mapping[:, :half], left[jnp.where(has_left, step, ITERS), part],
            preferred_element_type=jnp.float32)

        @pl.when(has_below)
        def _():
            to_above(step, part).wait_recv()

        arrived = below[jnp.where(has_below, step, ITERS), part]
        upper = (total[half:] + jnp.dot(
            mapping[half:, half:], arrived, preferred_element_type=jnp.float32)).astype(jnp.bfloat16)
        if last:
            traces[0, 0, half:, part * width:(part + 1) * width] = upper
        else:
            state[step + 1, part, half:] = upper

            @pl.when(has_above)
            def _():
                to_above(step + 1, part).start()

        if part == PARTS - 1 and not last:
            pass_on(step + 1, 0)
        elif part < PARTS - 1:
            pl.when(step > 0)(lambda: pass_on(step, part + 1))

        right = (total[:half] + jnp.dot(
            mapping[:half, half:], arrived, preferred_element_type=jnp.float32)).astype(jnp.bfloat16)
        if last:
            traces[0, 0, :half, part * width:(part + 1) * width] = right
        else:
            state[step + 1, part, :half] = right

            send_right(step + 1, part)

    def one_step(step, carry):
        for part in range(PARTS):
            advance(step, part, False)
        return carry

    lax.fori_loop(0, ITERS - 1, one_step, 0)
    for part in range(PARTS):
        advance(ITERS - 1, part, True)

    def drain(step, carry):
        for part in range(PARTS):
            @pl.when(has_above)
            def _():
                to_above(step, part).wait_send()

            @pl.when(has_right)
            def _():
                to_right(step, part).wait_send()

            for kind in range(len(PIECES)):
                @pl.when(passes[kind])
                def _():
                    from_seam(step, part, kind).wait_send()
        return carry

    lax.fori_loop(0, ITERS, drain, 0)


def per_device(rows, cols, trace_maps, sources):
    order, count = sources.shape[2:]
    half, width = order // 2, count // PARTS
    bf16, dma = jnp.bfloat16, pltpu.SemaphoreType.DMA
    return pl.pallas_call(
        functools.partial(kernel, rows, cols),
        out_shape=jax.ShapeDtypeStruct(sources.shape, bf16),
        in_specs=[pl.BlockSpec(memory_space=pltpu.HBM)] * 2,
        out_specs=pl.BlockSpec(memory_space=pltpu.VMEM),
        scratch_shapes=[
            pltpu.VMEM((order, order), bf16),
            pltpu.VMEM((ITERS, PARTS, order, width), bf16),
            pltpu.VMEM((ITERS + 1, PARTS, half, width), bf16),
            pltpu.VMEM((ITERS + 1, PARTS, half, width), bf16),
            pltpu.VMEM((ITERS, PARTS, max(piece[2] for piece in PIECES), width), bf16),
            pltpu.VMEM((order, width), jnp.float32),
            dma((PARTS,)),
            dma,
            dma((ITERS, PARTS)),
            dma((ITERS, PARTS)),
            dma((ITERS, PARTS)),
            dma((ITERS, PARTS)),
            dma((ITERS, PARTS)),
            dma((ITERS, PARTS)),
        ],
        compiler_params=pltpu.CompilerParams(
            collective_id=0, has_side_effects=True, vmem_limit_bytes=48 << 20),
    )(*(pltpu.with_memory_space_constraint(array, pltpu.HBM) for array in (trace_maps, sources)))


def solution(mesh):
    placed = P("row", "col", None, None)
    return jax.shard_map(
        functools.partial(per_device, mesh.shape["row"], mesh.shape["col"]),
        mesh=mesh,
        in_specs=(placed, placed),
        out_specs=placed,
        check_vma=False,
    )
```

```python
import functools

import jax
import jax.numpy as jnp
from jax import lax
from jax.experimental import pallas as pl
from jax.experimental.pallas import tpu as pltpu
from jax.sharding import PartitionSpec as P

ITERS = 8
RUN = 32
PIECES = ((0, 1, 96, 0, 1), (1, 3, 184, 96, 1), (3, 4, 176, 464, 1))
PARTS = 2
MESH = pl.DeviceIdType.MESH


def kernel(rows, cols, maps, sources, traces, mapping, state, left, below, seam, total,
           load_sem, map_sem, right_sent, up_sent, left_got, below_got, seam_sent, seam_got):
    half = left.shape[2]
    width = left.shape[3]
    row, col = lax.axis_index("row"), lax.axis_index("col")
    has_left, has_below = col > 0, row > 0
    has_right, has_above = col < cols - 1, row < rows - 1
    before_seam, after_seam = col == RUN - 1, col == RUN
    chip = (col - RUN) // 2
    passes = [(col % 2 == core) & (chip >= max(first, 1)) & (chip < end) for first, end, _, _, core in PIECES]
    on_seam = functools.reduce(jnp.logical_or, passes)

    def lanes(part):
        return pl.ds(part * width, width)

    loads = [pltpu.make_async_copy(sources.at[0, 0, :, lanes(part)], state.at[0, part], load_sem.at[part])
             for part in range(PARTS)]
    for load in loads:
        load.start()
    map_load = pltpu.make_async_copy(maps.at[0, 0], mapping, map_sem)
    map_load.start()

    barrier = pltpu.get_barrier_semaphore()

    @pl.when(has_left)
    def _():
        pl.semaphore_signal(barrier, inc=1, device_id={"col": col - 1}, device_id_type=MESH)

    @pl.when(has_below)
    def _():
        pl.semaphore_signal(barrier, inc=1, device_id={"row": row - 1}, device_id_type=MESH)

    @pl.when(on_seam)
    def _():
        pl.semaphore_signal(barrier, inc=1, device_id={"col": RUN - 1}, device_id_type=MESH)

    @pl.when(after_seam)
    def _():
        for first, end, _, _, core in PIECES:
            for other in range(max(first, 1), end):
                pl.semaphore_signal(barrier, inc=1, device_id={"col": RUN + core + 2 * other}, device_id_type=MESH)

    @pl.when(has_right | has_above | on_seam)
    def _():
        pl.semaphore_wait(barrier, has_right.astype(jnp.int32) + has_above.astype(jnp.int32)
                          + on_seam.astype(jnp.int32) + (sum(end - first for first, end, *_ in PIECES) - 1) * before_seam.astype(jnp.int32))

    def to_right(step, part):
        return pltpu.make_async_remote_copy(
            src_ref=state.at[step, part, pl.ds(0, half)], dst_ref=left.at[step, part],
            send_sem=right_sent.at[step, part], recv_sem=left_got.at[step, part],
            device_id={"col": lax.rem(col + 1, cols)}, device_id_type=MESH)

    def to_above(step, part):
        return pltpu.make_async_remote_copy(
            src_ref=state.at[step, part, pl.ds(half, half)], dst_ref=below.at[step, part],
            send_sem=up_sent.at[step, part], recv_sem=below_got.at[step, part],
            device_id={"row": lax.rem(row + 1, rows)}, device_id_type=MESH)

    def straight(step, part):
        tall = PIECES[0][2]
        return pltpu.make_async_remote_copy(
            src_ref=state.at[step, part, pl.ds(0, tall)], dst_ref=left.at[step, part, pl.ds(0, tall)],
            send_sem=right_sent.at[step, part], recv_sem=left_got.at[step, part],
            device_id={"col": RUN}, device_id_type=MESH)

    def rows_of(kind, other):
        first, _, tall, start, _ = PIECES[kind]
        return pl.ds(pl.multiple_of(start + (other - first) * tall, 8), tall)

    def to_seam(step, part, kind, other):
        return pltpu.make_async_remote_copy(
            src_ref=state.at[step, part, rows_of(kind, other)],
            dst_ref=seam.at[step, part, pl.ds(0, PIECES[kind][2])],
            send_sem=right_sent.at[step, part], recv_sem=seam_got.at[step, part],
            device_id={"col": RUN + PIECES[kind][4] + 2 * other}, device_id_type=MESH)

    def from_seam(step, part, kind):
        return pltpu.make_async_remote_copy(
            src_ref=seam.at[step, part, pl.ds(0, PIECES[kind][2])],
            dst_ref=left.at[step, part, rows_of(kind, chip)],
            send_sem=seam_sent.at[step, part], recv_sem=left_got.at[step, part],
            device_id={"col": RUN}, device_id_type=MESH)

    def send_right(step, part):
        @pl.when(has_right & jnp.logical_not(before_seam))
        def _():
            to_right(step, part).start()

        @pl.when(before_seam)
        def _():
            for kind in reversed(range(len(PIECES))):
                def send(other, carry):
                    to_seam(step, part, kind, other).start()
                    return carry

                lax.fori_loop(max(PIECES[kind][0], 1), PIECES[kind][1], send, 0)
            straight(step, part).start()

    def pass_on(step, part):
        for kind in range(len(PIECES)):
            @pl.when(passes[kind])
            def _():
                to_seam(step, part, kind, chip).wait_recv()
                from_seam(step, part, kind).start()

    for part in range(PARTS):
        loads[part].wait()

        @pl.when(has_above)
        def _():
            to_above(0, part).start()

        @pl.when(has_right)
        def _():
            to_right(0, part).start()

    @pl.when(jnp.logical_not(has_left))
    def _():
        left[ITERS] = jnp.zeros_like(left[ITERS])

    @pl.when(jnp.logical_not(has_below))
    def _():
        below[ITERS] = jnp.zeros_like(below[ITERS])

    map_load.wait()

    def advance(step, part, last):
        @pl.when(has_left)
        def _():
            to_right(step, part).wait_recv()

        total[...] = state[0, part].astype(jnp.float32) + jnp.dot(
            mapping[:, :half], left[jnp.where(has_left, step, ITERS), part],
            preferred_element_type=jnp.float32)

        if part == PARTS - 1 and not last:
            pass_on(step + 1, 0)
        elif part < PARTS - 1:
            pl.when(step > 0)(lambda: pass_on(step, part + 1))

        @pl.when(has_below)
        def _():
            to_above(step, part).wait_recv()

        arrived = below[jnp.where(has_below, step, ITERS), part]
        upper = (total[half:] + jnp.dot(
            mapping[half:, half:], arrived, preferred_element_type=jnp.float32)).astype(jnp.bfloat16)
        if last:
            traces[0, 0, half:, part * width:(part + 1) * width] = upper
        else:
            state[step + 1, part, half:] = upper

            @pl.when(has_above)
            def _():
                to_above(step + 1, part).start()

        right = (total[:half] + jnp.dot(
            mapping[:half, half:], arrived, preferred_element_type=jnp.float32)).astype(jnp.bfloat16)
        if last:
            traces[0, 0, :half, part * width:(part + 1) * width] = right
        else:
            state[step + 1, part, :half] = right

            send_right(step + 1, part)

    def one_step(step, carry):
        for part in range(PARTS):
            advance(step, part, False)
        return carry

    lax.fori_loop(0, ITERS - 1, one_step, 0)
    for part in range(PARTS):
        advance(ITERS - 1, part, True)

    def drain(step, carry):
        for part in range(PARTS):
            @pl.when(has_above)
            def _():
                to_above(step, part).wait_send()

            @pl.when(has_right)
            def _():
                to_right(step, part).wait_send()

            for kind in range(len(PIECES)):
                @pl.when(passes[kind] & (step > 0))
                def _():
                    from_seam(step, part, kind).wait_send()
        return carry

    lax.fori_loop(0, ITERS, drain, 0)


def per_device(rows, cols, trace_maps, sources):
    order, count = sources.shape[2:]
    half, width = order // 2, count // PARTS
    bf16, dma = jnp.bfloat16, pltpu.SemaphoreType.DMA
    return pl.pallas_call(
        functools.partial(kernel, rows, cols),
        out_shape=jax.ShapeDtypeStruct(sources.shape, bf16),
        in_specs=[pl.BlockSpec(memory_space=pltpu.HBM)] * 2,
        out_specs=pl.BlockSpec(memory_space=pltpu.VMEM),
        scratch_shapes=[
            pltpu.VMEM((order, order), bf16),
            pltpu.VMEM((ITERS, PARTS, order, width), bf16),
            pltpu.VMEM((ITERS + 1, PARTS, half, width), bf16),
            pltpu.VMEM((ITERS + 1, PARTS, half, width), bf16),
            pltpu.VMEM((ITERS, PARTS, max(piece[2] for piece in PIECES), width), bf16),
            pltpu.VMEM((order, width), jnp.float32),
            dma((PARTS,)),
            dma,
            dma((ITERS, PARTS)),
            dma((ITERS, PARTS)),
            dma((ITERS, PARTS)),
            dma((ITERS, PARTS)),
            dma((ITERS, PARTS)),
            dma((ITERS, PARTS)),
        ],
        compiler_params=pltpu.CompilerParams(
            collective_id=0, has_side_effects=True, vmem_limit_bytes=48 << 20),
    )(*(pltpu.with_memory_space_constraint(array, pltpu.HBM) for array in (trace_maps, sources)))


def solution(mesh):
    placed = P("row", "col", None, None)
    return jax.shard_map(
        functools.partial(per_device, mesh.shape["row"], mesh.shape["col"]),
        mesh=mesh,
        in_specs=(placed, placed),
        out_specs=placed,
        check_vma=False,
    )
```

```python
import functools

import jax
import jax.numpy as jnp
from jax import lax
from jax.experimental import pallas as pl
from jax.experimental.pallas import tpu as pltpu
from jax.sharding import PartitionSpec as P

ITERS = 8
RUN = 32
PIECES = ((0, 1, 96, 0, 1), (1, 3, 184, 96, 1), (3, 4, 176, 464, 1))
PARTS = 2
MESH = pl.DeviceIdType.MESH


def kernel(rows, cols, maps, sources, traces, mapping, state, left, below, seam, total,
           load_sem, map_sem, right_sent, up_sent, left_got, below_got, seam_sent, seam_got):
    half = left.shape[2]
    width = left.shape[3]
    row, col = lax.axis_index("row"), lax.axis_index("col")
    has_left, has_below = col > 0, row > 0
    has_right, has_above = col < cols - 1, row < rows - 1
    before_seam, after_seam = col == RUN - 1, col == RUN
    chip = (col - RUN) // 2
    passes = [(col % 2 == core) & (chip >= max(first, 1)) & (chip < end) for first, end, _, _, core in PIECES]
    on_seam = functools.reduce(jnp.logical_or, passes)

    def lanes(part):
        return pl.ds(part * width, width)

    barrier = pltpu.get_barrier_semaphore()

    @pl.when(has_left)
    def _():
        pl.semaphore_signal(barrier, inc=1, device_id={"col": col - 1}, device_id_type=MESH)

    @pl.when(has_below)
    def _():
        pl.semaphore_signal(barrier, inc=1, device_id={"row": row - 1}, device_id_type=MESH)

    @pl.when(on_seam)
    def _():
        pl.semaphore_signal(barrier, inc=1, device_id={"col": RUN - 1}, device_id_type=MESH)

    @pl.when(after_seam)
    def _():
        for first, end, _, _, core in PIECES:
            for other in range(max(first, 1), end):
                pl.semaphore_signal(barrier, inc=1, device_id={"col": RUN + core + 2 * other}, device_id_type=MESH)

    loads = [pltpu.make_async_copy(sources.at[0, 0, :, lanes(part)], state.at[0, part], load_sem.at[part])
             for part in range(PARTS)]
    for load in loads:
        load.start()

    @pl.when(has_right | has_above | on_seam)
    def _():
        pl.semaphore_wait(barrier, has_right.astype(jnp.int32) + has_above.astype(jnp.int32)
                          + on_seam.astype(jnp.int32) + (sum(end - first for first, end, *_ in PIECES) - 1) * before_seam.astype(jnp.int32))

    def to_right(step, part):
        return pltpu.make_async_remote_copy(
            src_ref=state.at[step, part, pl.ds(0, half)], dst_ref=left.at[step, part],
            send_sem=right_sent.at[step, part], recv_sem=left_got.at[step, part],
            device_id={"col": lax.rem(col + 1, cols)}, device_id_type=MESH)

    def to_above(step, part):
        return pltpu.make_async_remote_copy(
            src_ref=state.at[step, part, pl.ds(half, half)], dst_ref=below.at[step, part],
            send_sem=up_sent.at[step, part], recv_sem=below_got.at[step, part],
            device_id={"row": lax.rem(row + 1, rows)}, device_id_type=MESH)

    def straight(step, part):
        tall = PIECES[0][2]
        return pltpu.make_async_remote_copy(
            src_ref=state.at[step, part, pl.ds(0, tall)], dst_ref=left.at[step, part, pl.ds(0, tall)],
            send_sem=right_sent.at[step, part], recv_sem=left_got.at[step, part],
            device_id={"col": RUN}, device_id_type=MESH)

    def rows_of(kind, other):
        first, _, tall, start, _ = PIECES[kind]
        return pl.ds(pl.multiple_of(start + (other - first) * tall, 8), tall)

    def to_seam(step, part, kind, other):
        return pltpu.make_async_remote_copy(
            src_ref=state.at[step, part, rows_of(kind, other)],
            dst_ref=seam.at[step, part, pl.ds(0, PIECES[kind][2])],
            send_sem=right_sent.at[step, part], recv_sem=seam_got.at[step, part],
            device_id={"col": RUN + PIECES[kind][4] + 2 * other}, device_id_type=MESH)

    def from_seam(step, part, kind):
        return pltpu.make_async_remote_copy(
            src_ref=seam.at[step, part, pl.ds(0, PIECES[kind][2])],
            dst_ref=left.at[step, part, rows_of(kind, chip)],
            send_sem=seam_sent.at[step, part], recv_sem=left_got.at[step, part],
            device_id={"col": RUN}, device_id_type=MESH)

    def send_right(step, part):
        @pl.when(has_right & jnp.logical_not(before_seam))
        def _():
            to_right(step, part).start()

        @pl.when(before_seam)
        def _():
            for kind in reversed(range(len(PIECES))):
                def send(other, carry):
                    to_seam(step, part, kind, other).start()
                    return carry

                lax.fori_loop(max(PIECES[kind][0], 1), PIECES[kind][1], send, 0)
            straight(step, part).start()

    def pass_on(step, part):
        for kind in range(len(PIECES)):
            @pl.when(passes[kind])
            def _():
                to_seam(step, part, kind, chip).wait_recv()
                from_seam(step, part, kind).start()

    for part in range(PARTS):
        loads[part].wait()

        @pl.when(has_above)
        def _():
            to_above(0, part).start()

        @pl.when(has_right)
        def _():
            to_right(0, part).start()

    map_load = pltpu.make_async_copy(maps.at[0, 0], mapping, map_sem)
    map_load.start()

    @pl.when(jnp.logical_not(has_left))
    def _():
        left[ITERS] = jnp.zeros_like(left[ITERS])

    @pl.when(jnp.logical_not(has_below))
    def _():
        below[ITERS] = jnp.zeros_like(below[ITERS])

    map_load.wait()

    def advance(step, part, last):
        @pl.when(has_left)
        def _():
            to_right(step, part).wait_recv()

        total[...] = state[0, part].astype(jnp.float32) + jnp.dot(
            mapping[:, :half], left[jnp.where(has_left, step, ITERS), part],
            preferred_element_type=jnp.float32)

        if part == PARTS - 1 and not last:
            pass_on(step + 1, 0)
        elif part < PARTS - 1:
            pl.when(step > 0)(lambda: pass_on(step, part + 1))

        @pl.when(has_below)
        def _():
            to_above(step, part).wait_recv()

        arrived = below[jnp.where(has_below, step, ITERS), part]
        upper = (total[half:] + jnp.dot(
            mapping[half:, half:], arrived, preferred_element_type=jnp.float32)).astype(jnp.bfloat16)
        if last:
            traces[0, 0, half:, part * width:(part + 1) * width] = upper
        else:
            state[step + 1, part, half:] = upper

            @pl.when(has_above)
            def _():
                to_above(step + 1, part).start()

        right = (total[:half] + jnp.dot(
            mapping[:half, half:], arrived, preferred_element_type=jnp.float32)).astype(jnp.bfloat16)
        if last:
            traces[0, 0, :half, part * width:(part + 1) * width] = right
        else:
            state[step + 1, part, :half] = right

            send_right(step + 1, part)

    def one_step(step, carry):
        for part in range(PARTS):
            advance(step, part, False)
        return carry

    lax.fori_loop(0, ITERS - 1, one_step, 0)
    for part in range(PARTS):
        advance(ITERS - 1, part, True)

    def drain(step, carry):
        for part in range(PARTS):
            @pl.when(has_above)
            def _():
                to_above(step, part).wait_send()

            @pl.when(has_right)
            def _():
                to_right(step, part).wait_send()

            for kind in range(len(PIECES)):
                @pl.when(passes[kind] & (step > 0))
                def _():
                    from_seam(step, part, kind).wait_send()
        return carry

    lax.fori_loop(0, ITERS, drain, 0)


def per_device(rows, cols, trace_maps, sources):
    order, count = sources.shape[2:]
    half, width = order // 2, count // PARTS
    bf16, dma = jnp.bfloat16, pltpu.SemaphoreType.DMA
    return pl.pallas_call(
        functools.partial(kernel, rows, cols),
        out_shape=jax.ShapeDtypeStruct(sources.shape, bf16),
        in_specs=[pl.BlockSpec(memory_space=pltpu.HBM)] * 2,
        out_specs=pl.BlockSpec(memory_space=pltpu.VMEM),
        scratch_shapes=[
            pltpu.VMEM((order, order), bf16),
            pltpu.VMEM((ITERS, PARTS, order, width), bf16),
            pltpu.VMEM((ITERS + 1, PARTS, half, width), bf16),
            pltpu.VMEM((ITERS + 1, PARTS, half, width), bf16),
            pltpu.VMEM((ITERS, PARTS, max(piece[2] for piece in PIECES), width), bf16),
            pltpu.VMEM((order, width), jnp.float32),
            dma((PARTS,)),
            dma,
            dma((ITERS, PARTS)),
            dma((ITERS, PARTS)),
            dma((ITERS, PARTS)),
            dma((ITERS, PARTS)),
            dma((ITERS, PARTS)),
            dma((ITERS, PARTS)),
        ],
        compiler_params=pltpu.CompilerParams(
            collective_id=0, has_side_effects=True, vmem_limit_bytes=48 << 20),
    )(*(pltpu.with_memory_space_constraint(array, pltpu.HBM) for array in (trace_maps, sources)))


def solution(mesh):
    placed = P("row", "col", None, None)
    return jax.shard_map(
        functools.partial(per_device, mesh.shape["row"], mesh.shape["col"]),
        mesh=mesh,
        in_specs=(placed, placed),
        out_specs=placed,
        check_vma=False,
    )
```
